1024 devices in a mesh: row: 64 (over z, core), col: 16 (over y, x).
Axes of the slice: x: 4, y: 4, z: 32, core: 2. Of those that a mesh axis runs over, the one named last changes fastest.
Arguments:
- depth: float32 [4096, 2048], P('row', 'col'), may hold values from 0 to 12, as said below
- elevation: float32 [4096, 2048], P('row', 'col'), may hold values from -4 to 4
- flow_x: float32 [4096, 2048], P('row', 'col'), may hold values from -3 to 3
- flow_y: float32 [4096, 2048], P('row', 'col'), may hold values from -3 to 3
- wet_mask: int32 [4096, 2048], P('row', 'col'), may hold values 0 or 1
- manning_class: int32 [4096, 2048], P('row', 'col'), may hold values from 0 to 7
- manning_table: float32 [8], replicated, may hold values from 0.02 to 0.2
Outputs:
- depth_out: float32 [4096, 2048], P('row', 'col')
- flow_x_out: float32 [4096, 2048], P('row', 'col')
- flow_y_out: float32 [4096, 2048], P('row', 'col')
The draws below stay inside these ranges and needn't reach their ends.
Inputs may be any that keep to these rules, and one draw needn't show every extreme that they name: `depth`: depth is 0 or positive.
All inputs are finite; a program needn't handle non-finite values. No bound on the sum of `wet_mask` on one device may be relied on, other than what follows from the above.
Results may differ from the reference program's by a relative error of at most 0.000033.
Values sent between devices are 32-bit elements; how exact they have to be, the bound alone decides.
No kernel may reach another device: no remote copies, remote signals or barrier semaphores. Data moves between devices by JAX's collectives and lax.ppermute only.
A program may use at most 32 MiB of HBM per device.

```python
import math
import jax
import jax.numpy as jnp
from jax import lax

ITERS = 12
CLASSES = 8
NX = 4096
NY = 2048


def draw_depth(key, part):
    key_base = jax.random.fold_in(key, 11)
    key_dry = jax.random.fold_in(key, 12)
    row_frac = (jnp.arange(NX, dtype=jnp.float32) / NX)[:, None]
    col_frac = (jnp.arange(NY, dtype=jnp.float32) / NY)[None, :]
    base = jnp.exp(jax.random.uniform(key_base, (NX, NY), jnp.float32, jnp.log(0.05), 0.0))
    trend = (1.0 + 3.0 * row_frac) * (1.0 + 2.0 * col_frac)
    dry = jax.random.bernoulli(key_dry, 0.125, (NX, NY))
    return jnp.where(dry, 0.0, base * trend).astype(jnp.float32)


def plant(array, rng, low, top_value):
    extent = array.shape
    index_at = [jax.random.randint(jax.random.fold_in(rng, axis), (), 0, extent[axis]) for axis in range(len(extent))]
    array = array.at[tuple(index_at)].set(low)
    longest = extent.index(max(extent))
    index_at[longest] = (index_at[longest] + 1) % extent[longest]
    return array.at[tuple(index_at)].set(top_value)


def block_scale(rng, dims, split, low, largest):
    factor_of, own = 1.0, jax.random.fold_in(rng, 6)
    for position, blocks in split:
        steps = jnp.exp(jax.random.uniform(jax.random.fold_in(own, position), (blocks,), jnp.float32, low / len(split), largest / len(split)))
        factor_of = factor_of * jnp.repeat(steps, dims[position] // blocks).reshape([-1 if axis == position else 1 for axis in range(len(dims))])
    return factor_of


def bell_draw(rng, extent, spread, most, pieces=(), held_as=jnp.bfloat16):
    values = spread * jax.random.normal(rng, extent, jnp.float32)
    if pieces:
        values = values * block_scale(rng, extent, pieces, -0.22, 0.18)
    return jnp.clip(values, -most, most).astype(held_as)


def setup_inputs(seed: int = 0) -> dict:
    streams_of = jax.random.split(jax.random.key(seed), 8)
    depth = draw_depth(jax.random.fold_in(streams_of[7], 71), 0)
    elevation = bell_draw(streams_of[1], (NX, NY), 0.5, 4.0, ((0, 64), (1, 16)), jnp.float32)
    flow_x = bell_draw(streams_of[2], (NX, NY), 0.3, 3.0, ((0, 64), (1, 16)), jnp.float32)
    flow_y = bell_draw(streams_of[3], (NX, NY), 0.3, 3.0, ((0, 64), (1, 16)), jnp.float32)
    wet_mask = plant((jax.random.randint(streams_of[4], (NX, NY), 0, 8) < 7).astype(jnp.int32), jax.random.fold_in(streams_of[4], 1), 0, 1)
    manning_class = plant(jax.random.randint(streams_of[5], (NX, NY), 0, CLASSES), jax.random.fold_in(streams_of[5], 1), 0, CLASSES - 1).astype(jnp.int32)
    manning_table = jnp.clip(jnp.exp(jax.random.uniform(streams_of[6], (CLASSES,), jnp.float32, math.log(0.02), math.log(0.2))), 0.02, 0.2)
    return {"depth": depth, "elevation": elevation, "flow_x": flow_x, "flow_y": flow_y, "wet_mask": wet_mask, "manning_class": manning_class, "manning_table": manning_table}


GRAVITY = 9.81
SPACING = 30.0
COURANT = 0.7
DRY_FLOOR = 0.01
FLOW_FLOOR = 0.05

def face_flux(flow_old, surf_low, surf_high, bed_low, bed_high, rough_low, opening, time_step):
    flow_depth = jnp.maximum(surf_low, surf_high) - jnp.maximum(bed_low, bed_high)
    driving = jnp.maximum(flow_depth, 0.0)
    friction_depth = jnp.maximum(flow_depth, FLOW_FLOOR)
    slope = (surf_high - surf_low) / SPACING
    driven = flow_old - GRAVITY * driving * time_step * slope
    damping = 1.0 + GRAVITY * time_step * rough_low * jnp.abs(flow_old) / jnp.exp(7.0 / 3.0 * jnp.log(friction_depth))
    return opening * driven / damping

def reference(depth, elevation, flow_x, flow_y, wet_mask, manning_class, manning_table):
    rough_sq = jnp.zeros(depth.shape, depth.dtype)
    for class_id in range(CLASSES):
        rough_sq = rough_sq + jnp.where(manning_class == class_id, manning_table[class_id] * manning_table[class_id], 0.0)
    wet_open = wet_mask.astype(depth.dtype)
    bed = jnp.pad(elevation, 1)
    rough = jnp.pad(rough_sq, 1)
    opening = jnp.pad(wet_open, 1)

    def advance(counter, carry):
        depth_now, flow_rows, flow_cols = carry
        time_step = jnp.min(COURANT * SPACING / jnp.sqrt(GRAVITY * jnp.maximum(depth_now, DRY_FLOOR)))
        surface = jnp.pad(depth_now, 1) + bed
        row_old = jnp.pad(flow_rows, 1)
        col_old = jnp.pad(flow_cols, 1)
        rows_new = face_flux(row_old[:-1, 1:-1], surface[:-1, 1:-1], surface[1:, 1:-1], bed[:-1, 1:-1], bed[1:, 1:-1], rough[:-1, 1:-1], opening[:-1, 1:-1] * opening[1:, 1:-1], time_step)
        cols_new = face_flux(col_old[1:-1, :-1], surface[1:-1, :-1], surface[1:-1, 1:], bed[1:-1, :-1], bed[1:-1, 1:], rough[1:-1, :-1], opening[1:-1, :-1] * opening[1:-1, 1:], time_step)
        change = rows_new[:-1] - rows_new[1:] + (cols_new[:, :-1] - cols_new[:, 1:])
        depth_next = jnp.maximum(depth_now + time_step / SPACING * change, 0.0)
        return (depth_next, rows_new[1:], cols_new[:, 1:])
    depth_out, flow_x_out, flow_y_out = lax.fori_loop(0, ITERS, advance, (depth, flow_x, flow_y))
    return (depth_out, flow_x_out, flow_y_out)
```

```python
import jax
import jax.numpy as jnp
from jax import lax
from jax.experimental import pallas as pl
from jax.experimental.pallas import tpu as pltpu
from jax.sharding import PartitionSpec as P

ITERS = 12
CLASSES = 8
HALO = ITERS

GRAVITY = 9.81
SPACING = 30.0
COURANT = 0.7
DRY_FLOOR = 0.01
FLOW_FLOOR = 0.05


def neighbours(axis):
    peers = lax.axis_size(axis)
    up = [(i, i + 1) for i in range(peers - 1)]
    down = [(j, i) for i, j in up]
    return up, down


def with_halo(fields):
    rows, cols = fields.shape[1:]
    up, down = neighbours("row")
    before = lax.ppermute(fields[:, rows - HALO :], "row", up)
    after = lax.ppermute(fields[:, :HALO], "row", down)
    fields = jnp.concatenate([fields, after, before], axis=1)
    up, down = neighbours("col")
    before = lax.ppermute(fields[:, :, cols - HALO :], "col", up)
    after = lax.ppermute(fields[:, :, :HALO], "col", down)
    gap = jnp.zeros((*fields.shape[:2], cols - 2 * HALO), fields.dtype)
    return jnp.concatenate([fields, after, gap, before], axis=2)


def next_of(x, axis):
    return pltpu.roll(x, x.shape[axis] - 1, axis)


def previous_of(x, axis):
    return pltpu.roll(x, 1, axis)


def face_flux(flow_old, surface, surf_high, bed_max, rough, opening, time_step):
    flow_depth = jnp.maximum(surface, surf_high) - bed_max
    driving = jnp.maximum(flow_depth, 0.0)
    friction_depth = jnp.maximum(flow_depth, FLOW_FLOOR)
    slope = (surf_high - surface) / SPACING
    driven = flow_old - GRAVITY * driving * time_step * slope
    damping = 1.0 + GRAVITY * time_step * rough * jnp.abs(flow_old) * jnp.exp(
        -7.0 / 3.0 * jnp.log(friction_depth)
    )
    return opening * driven / damping


def step_kernel(tile, gathered, state, fixed, state_out, bound_out):
    deepest = jnp.max(gathered[...], axis=(0, 1), keepdims=True)
    time_step = COURANT * SPACING / jnp.sqrt(GRAVITY * jnp.maximum(deepest, DRY_FLOOR))
    depth = state[0]
    bed = fixed[0]
    rough = fixed[1]
    opening = fixed[2]
    surface = depth + bed
    flows = []
    for axis in (0, 1):
        flows.append(
            face_flux(
                state[1 + axis],
                surface,
                next_of(surface, axis),
                jnp.maximum(bed, next_of(bed, axis)),
                rough,
                opening * next_of(opening, axis),
                time_step,
            )
        )
    rows_new, cols_new = flows
    change = previous_of(rows_new, 0) - rows_new + (previous_of(cols_new, 1) - cols_new)
    depth = jnp.maximum(depth + time_step / SPACING * change, 0.0)
    state_out[0] = depth
    state_out[1] = rows_new
    state_out[2] = cols_new
    rows, cols = tile
    own = jnp.max(depth[:rows, :cols], axis=(0, 1), keepdims=True)
    bound_out[...] = jnp.broadcast_to(own, bound_out.shape)


def per_device(depth, elevation, flow_x, flow_y, wet_mask, manning_class, manning_table):
    rough_sq = jnp.zeros(depth.shape, jnp.float32)
    for class_id in range(CLASSES):
        rough_sq = rough_sq + jnp.where(
            manning_class == class_id, manning_table[class_id] * manning_table[class_id], 0.0
        )
    wet_open = wet_mask.astype(jnp.float32)
    rows, cols = depth.shape
    row_peers, col_peers = lax.axis_size("row"), lax.axis_size("col")
    padded = with_halo(jnp.stack([depth, flow_x, flow_y, elevation, rough_sq, wet_open]))
    state, fixed = padded[:3], padded[3:]

    def everywhere(bound):
        over_col = lax.all_to_all(bound, "col", 0, 0, tiled=True)
        merged = jnp.max(over_col, axis=0, keepdims=True)
        return lax.all_to_all(jnp.broadcast_to(merged, (row_peers, 128)), "row", 0, 0, tiled=True)

    step = pl.pallas_call(
        lambda *refs: step_kernel((rows, cols), *refs),
        out_shape=(
            jax.ShapeDtypeStruct(state.shape, jnp.float32),
            jax.ShapeDtypeStruct((col_peers, 128), jnp.float32),
        ),
        name="flood_step",
    )
    bound = jnp.broadcast_to(jnp.max(depth), (col_peers, 128))

    def one_round(counter, carry):
        state, bound = carry
        return step(everywhere(bound), state, fixed)

    state, bound = lax.fori_loop(0, ITERS, one_round, (state, bound))
    final = state[:, :rows, :cols]
    return (final[0], final[1], final[2])


def solution(mesh):
    in_specs = (
        P("row", "col"),
        P("row", "col"),
        P("row", "col"),
        P("row", "col"),
        P("row", "col"),
        P("row", "col"),
        P(),
    )
    out_specs = (P("row", "col"), P("row", "col"), P("row", "col"))
    return jax.shard_map(
        per_device, mesh=mesh, in_specs=in_specs, out_specs=out_specs, check_vma=False
    )
```

```python
import jax
import jax.numpy as jnp
from jax import lax
from jax.experimental import pallas as pl
from jax.experimental.pallas import tpu as pltpu
from jax.sharding import PartitionSpec as P

ITERS = 12
CLASSES = 8
HALO = ITERS

GRAVITY = 9.81
SPACING = 30.0
COURANT = 0.7
DRY_FLOOR = 0.01
FLOW_FLOOR = 0.05

NOTE = 256
KEYS = (12, 13)
NEAR_AT = 48
FAR_LAST_AT = 16
FAR_AT = 128
FIELDS = 6


def neighbours(axis):
    peers = lax.axis_size(axis)
    up = [(i, i + 1) for i in range(peers - 1)]
    down = [(j, i) for i, j in up]
    return up, down


def with_halo(fields):
    rows, cols = fields.shape[1:]
    up, down = neighbours("row")
    before = lax.ppermute(fields[:, rows - HALO :], "row", up)
    after = lax.ppermute(fields[:, :HALO], "row", down)
    fields = jnp.concatenate([fields, after, before], axis=1)
    up, down = neighbours("col")
    before = lax.ppermute(fields[:, :, cols - HALO :], "col", up)
    after = lax.ppermute(fields[:, :, :HALO], "col", down)
    gap = jnp.zeros((*fields.shape[:2], cols - 2 * HALO), fields.dtype)
    return jnp.concatenate([fields, after, gap, before], axis=2)


def next_of(x, axis):
    return pltpu.roll(x, x.shape[axis] - 1, axis)


def previous_of(x, axis):
    return pltpu.roll(x, 1, axis)


def step_of(deepest):
    return COURANT * SPACING / jnp.sqrt(GRAVITY * jnp.maximum(deepest, DRY_FLOOR))


def fixed_parts(bed, opening):
    return tuple(
        (jnp.maximum(bed, next_of(bed, axis)), opening * next_of(opening, axis)) for axis in (0, 1)
    )


def face_flux(flow_old, surface, surf_high, bed_max, rough, opening, time_step):
    flow_depth = jnp.maximum(surface, surf_high) - bed_max
    driving = jnp.maximum(flow_depth, 0.0)
    friction_depth = jnp.maximum(flow_depth, FLOW_FLOOR)
    slope = (surf_high - surface) / SPACING
    driven = flow_old - GRAVITY * driving * time_step * slope
    damping = 1.0 + GRAVITY * time_step * rough * jnp.abs(flow_old) * jnp.exp(
        -7.0 / 3.0 * jnp.log(friction_depth)
    )
    return opening * driven / damping


def advance(depth, flow_x, flow_y, bed, rough, faces, time_step):
    surface = depth + bed
    (bed_x, open_x), (bed_y, open_y) = faces
    rows_new = face_flux(flow_x, surface, next_of(surface, 0), bed_x, rough, open_x, time_step)
    cols_new = face_flux(flow_y, surface, next_of(surface, 1), bed_y, rough, open_y, time_step)
    change = previous_of(rows_new, 0) - rows_new + (previous_of(cols_new, 1) - cols_new)
    return jnp.maximum(depth + time_step / SPACING * change, 0.0), rows_new, cols_new


def lanes_of(shape):
    return lax.broadcasted_iota(jnp.int32, shape, len(shape) - 1)


def rows_of(shape):
    return lax.broadcasted_iota(jnp.int32, shape, len(shape) - 2)


def total(x, how):
    return how(how(x, axis=0, keepdims=True), axis=1, keepdims=True)


def merged(notes):
    lane = lanes_of(notes.shape)
    out_lane = lanes_of((1, NOTE))
    place = rows_of((notes.shape[0], 1)).astype(jnp.float32)
    out = jnp.max(notes, axis=0, keepdims=True)
    near = (out_lane >= NEAR_AT) & (out_lane < FAR_AT)
    far = (out_lane >= FAR_AT) | ((out_lane >= FAR_LAST_AT) & (out_lane < NEAR_AT))
    for key, where in zip(KEYS, (near, far)):
        keyed = jnp.max(jnp.where(lane == key, notes, -1.0), axis=1, keepdims=True)
        best = keyed == jnp.max(keyed, axis=0, keepdims=True)
        first = jnp.min(jnp.where(best, place, 1e6), axis=0, keepdims=True)
        chosen = jnp.sum(jnp.where(place == first, notes, 0.0), axis=0, keepdims=True)
        out = jnp.where(where, chosen, out)
    return out


def merge_kernel(notes, out):
    out[...] = jnp.broadcast_to(merged(notes[:, 0, :])[:, None, :], out.shape)


def window_fields(note, reach):
    width = 2 * reach + 1
    span = width * FIELDS
    row, lane = rows_of((8, 128)), lanes_of((8, 128))
    packed = jnp.zeros((8, 128), jnp.float32)
    for i in range(width):
        if reach == 1:
            line, at = note[:, :128], NEAR_AT + span * i
        elif i < 4:
            line, at = note[:, FAR_AT:], span * i
        else:
            line, at = note[:, :128], FAR_LAST_AT
        line = jnp.broadcast_to(line, (8, 128))
        packed = jnp.where(row == i, pltpu.roll(line, (128 - at) % 128, 1), packed)
    inside = (row < width) & (lane < width)
    return [
        jnp.where(inside, pltpu.roll(packed, (128 - width * f) % 128, 1), 0.0) for f in range(FIELDS)
    ]


def packed_window(saved, at_row, at_col, reach):
    width = 2 * reach + 1
    span = width * FIELDS
    lane = lanes_of((8, 128))
    line_lane = lanes_of((1, 128))
    packed = jnp.zeros((8, 128), jnp.float32)
    top = at_row + 8 - reach
    off = lax.rem(top, 8)
    for f in range(FIELDS):
        strip = saved[f, pl.ds(pl.multiple_of(top - off, 8), 16), :]
        strip = pltpu.roll(strip, lax.rem(16 - off, 16), 0)[:8]
        shift = lax.rem(width * f + reach - at_col + 2 * 256, 256)
        moved = pltpu.roll(strip, shift, 1)[:, :128]
        packed = jnp.where((lane >= width * f) & (lane < width * (f + 1)), moved, packed)
    low = jnp.zeros((1, 128), jnp.float32)
    high = jnp.zeros((1, 128), jnp.float32)
    for i in range(width):
        line = packed[i : i + 1]
        if reach == 1:
            at = NEAR_AT + span * i
        elif i < 4:
            at = span * i
        else:
            at = FAR_LAST_AT
        moved = pltpu.roll(line, at, 1) if at else line
        here = (line_lane >= at) & (line_lane < at + span)
        if reach == 2 and i < 4:
            high = jnp.where(here, moved, high)
        else:
            low = jnp.where(here, moved, low)
    return low, high


def run_kernel(tile, first, *refs):
    if first:
        fields, depth_out, flow_x_out, flow_y_out, note_out, guess_out, known_out = refs[:7]
    else:
        notes, guess_in, known_in, fields, depth_out, flow_x_out, flow_y_out, note_out, guess_out, known_out = refs[:10]
    state, faces, saved, guesses, depths, spots = refs[-6:]
    rows, cols = tile
    line_lane = lanes_of((1, 128))

    if first:
        known = jnp.int32(-1)
        guess_out[...] = jnp.full((1, 128), -1.0, jnp.float32)
    else:
        note = merged(notes[:, 0, :])
        true = note[:, :128]
        old = guess_in[...]
        wrong = jnp.where((true != old) & (line_lane < ITERS), line_lane.astype(jnp.float32), 1.0 * ITERS)
        miss = jnp.min(wrong).astype(jnp.int32)
        before = known_in[0]
        held = miss > before
        guess = true
        pick = jnp.broadcast_to(line_lane == before + 1, (1, 128))
        ahead = jnp.max(jnp.where(pick, true, 0.0), axis=1, keepdims=True)
        windows = {reach: window_fields(note, reach) for reach in (1, 2)}
        faces_of = {reach: fixed_parts(w[3], w[5]) for reach, w in windows.items()}

        def moved(reach, deepest, now):
            w = windows[reach]
            return advance(*now, w[3], w[4], faces_of[reach], step_of(deepest))

        def centre(reach, depth):
            here = (rows_of((8, 128)) == reach) & (lanes_of((8, 128)) == reach)
            return total(jnp.where(here, depth, 0.0), jnp.max)

        near = moved(1, ahead, windows[1][:3])
        far = moved(2, ahead, windows[2][:3])
        second = centre(1, near[0])
        far = moved(2, second, far)
        third = centre(2, far[0])
        use = held & (line_lane == before + 2) & (second > 0.0)
        guess = jnp.where(use, second, guess)
        use = held & (line_lane == before + 3) & (third > 0.0)
        guess = jnp.where(use, third, guess)
        known = jnp.where(held, jnp.maximum(before + 3, miss), miss)
        guess_out[...] = guess
        square = (16, 128)
        onto = rows_of(square) == lanes_of(square)
        spread = jnp.sum(jnp.where(onto, jnp.broadcast_to(guess, square), 0.0), axis=1, keepdims=True)
        guesses[...] = jnp.broadcast_to(spread, square)
    known_out[0] = known

    for f in range(3):
        state[f] = fields[f]
    bed, rough, opening = fields[3], fields[4], fields[5]
    for axis, (bed_max, both) in enumerate(fixed_parts(bed, opening)):
        faces[2 * axis] = bed_max
        faces[2 * axis + 1] = both
    last = fields.shape[1] - 8
    for f in range(3, FIELDS):
        saved[f, :8] = fields[f, last:]
        saved[f, 8:] = fields[f]
    depths[...] = jnp.full(depths.shape, -1.0, jnp.float32)

    def one_step(step, carry):
        depth, flow_x, flow_y = state[0], state[1], state[2]
        own = depth[:rows, :cols]
        deepest = total(own, jnp.max)
        depths[pl.ds(step, 1), :] = jnp.broadcast_to(deepest, (1, 128))

        @pl.when(step == known + 1)
        def _():
            for f in range(3):
                saved[f, :8] = state[f, last:]
                saved[f, 8:] = state[f]

        for j in (0, 1):

            @pl.when(step == known + 2 + j)
            def _():
                cell = (rows_of((rows, cols)) * cols + lanes_of((rows, cols))).astype(jnp.float32)
                spots[j] = jnp.min(jnp.where(own == deepest, cell, 1.0 * (rows * cols - 1))).astype(jnp.int32)

        level = deepest if first else guesses[pl.ds(step, 1), :][:, :1]
        new = advance(
            depth,
            flow_x,
            flow_y,
            fields[3],
            fields[4],
            ((faces[0], faces[1]), (faces[2], faces[3])),
            step_of(level),
        )
        for f in range(3):
            state[f] = new[f]
        return carry

    spots[0] = 0
    spots[1] = 0
    lax.fori_loop(0, ITERS, one_step, 0)
    depth_out[...] = state[0, :rows, :cols]
    flow_x_out[...] = state[1, :rows, :cols]
    flow_y_out[...] = state[2, :rows, :cols]

    square = depths.shape
    onto = rows_of(square) == lanes_of(square)
    low = jnp.sum(jnp.where(onto, depths[...], 0.0), axis=0, keepdims=True)
    for j in (0, 1):
        key = jnp.max(jnp.where(line_lane == known + 2 + j, low, -1.0), axis=1, keepdims=True)
        low = jnp.where(line_lane == KEYS[j], key, low)
    near_low, _ = packed_window(saved, spots[0] // cols, lax.rem(spots[0], cols), 1)
    far_low, high = packed_window(saved, spots[1] // cols, lax.rem(spots[1], cols), 2)
    low = jnp.where((line_lane >= NEAR_AT) & (line_lane < NEAR_AT + 54), near_low, low)
    low = jnp.where((line_lane >= FAR_LAST_AT) & (line_lane < FAR_LAST_AT + 30), far_low, low)
    note = jnp.concatenate([low, high], axis=1)
    note_out[...] = jnp.broadcast_to(note[:, None, :], note_out.shape)


def per_device(depth, elevation, flow_x, flow_y, wet_mask, manning_class, manning_table):
    rough_sq = jnp.zeros(depth.shape, jnp.float32)
    for class_id in range(CLASSES):
        rough_sq = rough_sq + jnp.where(
            manning_class == class_id, manning_table[class_id] * manning_table[class_id], 0.0
        )
    wet_open = wet_mask.astype(jnp.float32)
    tile = depth.shape
    row_peers, col_peers = lax.axis_size("row"), lax.axis_size("col")
    fields = with_halo(jnp.stack([depth, flow_x, flow_y, elevation, rough_sq, wet_open]))
    large = fields.shape[1:]

    def f32(*shape):
        return jax.ShapeDtypeStruct(shape, jnp.float32)

    merge = pl.pallas_call(merge_kernel, out_shape=f32(row_peers, 1, NOTE), name="merge_notes")

    def everywhere(note):
        over_col = lax.all_to_all(note, "col", 0, 0, tiled=True)
        return lax.all_to_all(merge(over_col), "row", 0, 0, tiled=True)

    def run(first):
        vmem = pl.BlockSpec(memory_space=pltpu.VMEM)
        smem = pl.BlockSpec(memory_space=pltpu.SMEM)
        return pl.pallas_call(
            lambda *refs: run_kernel(tile, first, *refs),
            in_specs=[vmem] if first else [vmem, vmem, smem, vmem],
            out_shape=(
                f32(*tile),
                f32(*tile),
                f32(*tile),
                f32(col_peers, 1, NOTE),
                f32(1, 128),
                jax.ShapeDtypeStruct((1,), jnp.int32),
            ),
            out_specs=(vmem, vmem, vmem, vmem, vmem, smem),
            scratch_shapes=[
                pltpu.VMEM((3, *large), jnp.float32),
                pltpu.VMEM((4, *large), jnp.float32),
                pltpu.VMEM((FIELDS, large[0] + 8, large[1]), jnp.float32),
                pltpu.VMEM((16, 128), jnp.float32),
                pltpu.VMEM((16, 128), jnp.float32),
                pltpu.SMEM((2,), jnp.int32),
            ],
            name="first_run" if first else "later_run",
        )

    def settled(notes, guess):
        true = jnp.max(notes[:, 0, :ITERS], axis=0)
        return jnp.all(true == guess[0, :ITERS])

    *result, note, guess, known = run(True)(fields)
    again = run(False)

    def unsettled(carry):
        return jnp.logical_not(carry[1]) & (carry[0] <= ITERS)

    def one_round(carry):
        count, _, notes, guess, known, _ = carry
        *result, note, guess, known = again(notes, guess, known, fields)
        notes = everywhere(note)
        return count + 1, settled(notes, guess), notes, guess, known, tuple(result)

    carry = (jnp.int32(0), jnp.bool_(False), everywhere(note), guess, known, tuple(result))
    return lax.while_loop(unsettled, one_round, carry)[-1]


def solution(mesh):
    in_specs = (
        P("row", "col"),
        P("row", "col"),
        P("row", "col"),
        P("row", "col"),
        P("row", "col"),
        P("row", "col"),
        P(),
    )
    out_specs = (P("row", "col"), P("row", "col"), P("row", "col"))
    return jax.shard_map(
        per_device, mesh=mesh, in_specs=in_specs, out_specs=out_specs, check_vma=False
    )
```

```python
import jax
import jax.numpy as jnp
from jax import lax
from jax.experimental import pallas as pl
from jax.experimental.pallas import tpu as pltpu
from jax.sharding import PartitionSpec as P

ITERS = 12
CLASSES = 8
HALO = ITERS

GRAVITY = 9.81
SPACING = 30.0
COURANT = 0.7
DRY_FLOOR = 0.01
FLOW_FLOOR = 0.05

ROW = ("z", "core")

REACH = 4
FIELDS = 6
KEYS = ITERS


def note_places():
    room = [ITERS + REACH]
    places = {}
    for window in range(REACH, 0, -1):
        span = FIELDS * (2 * window + 1)
        for row in range(window + 1):
            tile = next((t for t, used in enumerate(room) if used + span <= 128), len(room))
            if tile == len(room):
                room.append(0)
            places[window, row] = (tile, room[tile])
            room[tile] += span
    return places, len(room)


PLACES, TILES = note_places()
NOTE = 128 * TILES


def neighbours(axis):
    peers = lax.axis_size(axis)
    up = [(i, i + 1) for i in range(peers - 1)]
    down = [(j, i) for i, j in up]
    return up, down


def with_halo(fields):
    rows, cols = fields.shape[1:]
    up, down = neighbours(ROW)
    before = lax.ppermute(fields[:, rows - HALO :], ROW, up)
    after = lax.ppermute(fields[:, :HALO], ROW, down)
    fields = jnp.concatenate([fields, after, before], axis=1)
    up, down = neighbours("col")
    before = lax.ppermute(fields[:, :, cols - HALO :], "col", up)
    after = lax.ppermute(fields[:, :, :HALO], "col", down)
    gap = jnp.zeros((*fields.shape[:2], cols - 2 * HALO), fields.dtype)
    return jnp.concatenate([fields, after, gap, before], axis=2)


def next_of(x, axis):
    return pltpu.roll(x, x.shape[axis] - 1, axis)


def previous_of(x, axis):
    return pltpu.roll(x, 1, axis)


def step_of(deepest):
    return COURANT * SPACING / jnp.sqrt(GRAVITY * jnp.maximum(deepest, DRY_FLOOR))


def fixed_parts(bed, opening):
    return tuple(
        (jnp.maximum(bed, next_of(bed, axis)), opening * next_of(opening, axis)) for axis in (0, 1)
    )


def face_flux(flow_old, surface, surf_high, bed_max, rough, opening, time_step):
    flow_depth = jnp.maximum(surface, surf_high) - bed_max
    driving = jnp.maximum(flow_depth, 0.0)
    friction_depth = jnp.maximum(flow_depth, FLOW_FLOOR)
    slope = (surf_high - surface) / SPACING
    driven = flow_old - GRAVITY * driving * time_step * slope
    damping = 1.0 + GRAVITY * time_step * rough * jnp.abs(flow_old) * jnp.exp(
        -7.0 / 3.0 * jnp.log(friction_depth)
    )
    return opening * driven / damping


def advance(depth, flow_x, flow_y, bed, rough, faces, time_step):
    surface = depth + bed
    (bed_x, open_x), (bed_y, open_y) = faces
    rows_new = face_flux(flow_x, surface, next_of(surface, 0), bed_x, rough, open_x, time_step)
    cols_new = face_flux(flow_y, surface, next_of(surface, 1), bed_y, rough, open_y, time_step)
    change = previous_of(rows_new, 0) - rows_new + (previous_of(cols_new, 1) - cols_new)
    return jnp.maximum(depth + time_step / SPACING * change, 0.0), rows_new, cols_new


def lanes_of(shape):
    return lax.broadcasted_iota(jnp.int32, shape, len(shape) - 1)


def rows_of(shape):
    return lax.broadcasted_iota(jnp.int32, shape, len(shape) - 2)


def total(x, how):
    return how(how(x, axis=0, keepdims=True), axis=1, keepdims=True)


def merged(notes):
    head = notes[:, :128]
    lane = lanes_of(head.shape)
    out_lane = lanes_of((1, NOTE))
    place = rows_of((notes.shape[0], 1)).astype(jnp.float32)
    out = jnp.max(notes, axis=0, keepdims=True)
    for window in range(1, REACH + 1):
        keyed = jnp.max(jnp.where(lane == KEYS + window - 1, head, -1.0), axis=1, keepdims=True)
        best = keyed == jnp.max(keyed, axis=0, keepdims=True)
        first = jnp.min(jnp.where(best, place, 1e6), axis=0, keepdims=True)
        chosen = jnp.sum(jnp.where(place == first, notes, 0.0), axis=0, keepdims=True)
        for row in range(window + 1):
            tile, at = PLACES[window, row]
            start = 128 * tile + at
            here = (out_lane >= start) & (out_lane < start + FIELDS * (2 * window + 1))
            out = jnp.where(here, chosen, out)
    return out


def merge_kernel(notes, out):
    out[...] = jnp.broadcast_to(merged(notes[:, 0, :])[:, None, :], out.shape)


def turned(x, shift, axis):
    size = x.shape[axis]
    return pltpu.roll(x, shift % size, axis) if shift % size else x


def window_shape(window):
    return (8 if 2 * window < 8 else 16, 128)


def columns_of(shape, width):
    lane = lanes_of(shape)
    column = lane
    for f in range(1, FIELDS):
        column = jnp.where(lane >= width * f, lane - width * f, column)
    return column


def window_fields(note, window):
    width = 2 * window + 1
    shape = window_shape(window)
    row, lane = rows_of(shape), lanes_of(shape)
    column = columns_of(shape, width)
    folded = jnp.zeros(shape, jnp.float32)
    for i in range(window + 1):
        tile, at = PLACES[window, i]
        line = turned(note[:, 128 * tile : 128 * (tile + 1)], -at, 1)
        folded = jnp.where(row == i, jnp.broadcast_to(line, shape), folded)
    lower = turned(folded, window + 1, 0)
    lower = jnp.where(column <= window, turned(lower, -window, 1), turned(lower, window + 1, 1))
    packed = jnp.where(row <= window, folded, lower)
    inside = jnp.abs(column - window) + jnp.abs(row - window) <= window
    packed = jnp.where(inside, packed, 0.0)
    return [jnp.where(lane < width, turned(packed, -width * f, 1), 0.0) for f in range(FIELDS)]


def window_lines(saved, at_row, at_col, window):
    width = 2 * window + 1
    shape = window_shape(window)
    row, lane = rows_of(shape), lanes_of(shape)
    column = columns_of(shape, width)
    packed = jnp.zeros(shape, jnp.float32)
    top = at_row + 8 - window
    off = lax.rem(top, 8)
    height = shape[0] + 8
    for f in range(FIELDS):
        strip = saved[f, pl.ds(pl.multiple_of(top - off, 8), height), :]
        strip = pltpu.roll(strip, lax.rem(height - off, height), 0)[: shape[0]]
        shift = lax.rem(width * f + window - at_col + 2 * 256, 256)
        moved = pltpu.roll(strip, shift, 1)[:, :128]
        packed = jnp.where((lane >= width * f) & (lane < width * (f + 1)), moved, packed)
    lower = turned(packed, -(window + 1), 0)
    lower = jnp.where(column > window, turned(lower, window, 1), turned(lower, -(window + 1), 1))
    folded = jnp.where(jnp.abs(column - window) <= row, packed, lower)
    return [folded[i : i + 1] for i in range(window + 1)]


def run_kernel(tile, first, certain, *refs):
    if first:
        fields, depth_out, flow_x_out, flow_y_out, note_out, guess_out, known_out = refs[:7]
    else:
        notes, guess_in, known_in, fields, depth_out, flow_x_out, flow_y_out, note_out, guess_out, known_out = refs[:10]
    state, faces, saved, guesses, depths, spots = refs[-6:]
    rows, cols = tile
    line_lane = lanes_of((1, 128))

    if first:
        known = jnp.int32(-1)
        guess_out[...] = jnp.full((1, 128), -1.0, jnp.float32)
    else:
        note = merged(notes[:, 0, :])
        true = note[:, :128]
        old = guess_in[...]
        wrong = jnp.where((true != old) & (line_lane < ITERS), line_lane.astype(jnp.float32), 1.0 * ITERS)
        miss = jnp.min(wrong).astype(jnp.int32)
        before = known_in[0]
        held = miss > before
        guess = true
        windows = {w: window_fields(note, w) for w in range(1, REACH + 1)}
        walls = {w: fixed_parts(parts[3], parts[5]) for w, parts in windows.items()}
        moving = {w: parts[:3] for w, parts in windows.items()}
        for stage in range(1, REACH + 1):
            level = jnp.max(jnp.where(line_lane == before + stage, guess, 0.0), axis=1, keepdims=True)
            time_step = step_of(level)
            for w in range(stage, REACH + 1):
                moving[w] = advance(*moving[w], windows[w][3], windows[w][4], walls[w], time_step)
            shape = window_shape(stage)
            here = (rows_of(shape) == stage) & (lanes_of(shape) == stage)
            centre = total(jnp.where(here, moving[stage][0], 0.0), jnp.max)
            target = before + stage + 1
            use = held & (target > miss) & (line_lane == target) & (centre > 0.0)
            guess = jnp.where(use, centre, guess)
        known = miss
        if not certain:
            known = jnp.where(held, jnp.maximum(before + REACH + 1, miss), miss)
        guess_out[...] = guess
        square = (16, 128)
        onto = rows_of(square) == lanes_of(square)
        spread = jnp.sum(jnp.where(onto, jnp.broadcast_to(guess, square), 0.0), axis=1, keepdims=True)
        guesses[...] = jnp.broadcast_to(spread, square)
    known_out[0] = known

    for f in range(3):
        state[f] = fields[f]
    bed, rough, opening = fields[3], fields[4], fields[5]
    for axis, (bed_max, both) in enumerate(fixed_parts(bed, opening)):
        faces[2 * axis] = bed_max
        faces[2 * axis + 1] = both
    last = fields.shape[1] - 8
    for f in range(3, FIELDS):
        saved[f, :8] = fields[f, last:]
        saved[f, 8:] = fields[f]
    depths[...] = jnp.full(depths.shape, -1.0, jnp.float32)

    def one_step(step, carry):
        depth, flow_x, flow_y = state[0], state[1], state[2]
        own = depth[:rows, :cols]
        deepest = total(own, jnp.max)
        depths[pl.ds(step, 1), :] = jnp.broadcast_to(deepest, (1, 128))

        @pl.when(step == known + 1)
        def _():
            for f in range(3):
                saved[f, :8] = state[f, last:]
                saved[f, 8:] = state[f]

        for j in range(REACH):

            @pl.when(step == known + 2 + j)
            def _():
                cell = (rows_of((rows, cols)) * cols + lanes_of((rows, cols))).astype(jnp.float32)
                spots[j] = jnp.min(jnp.where(own == deepest, cell, 1.0 * (rows * cols - 1))).astype(jnp.int32)

        level = deepest if first else guesses[pl.ds(step, 1), :][:, :1]
        new = advance(
            depth,
            flow_x,
            flow_y,
            fields[3],
            fields[4],
            ((faces[0], faces[1]), (faces[2], faces[3])),
            step_of(level),
        )
        for f in range(3):
            state[f] = new[f]
        return carry

    for j in range(REACH):
        spots[j] = 0
    lax.fori_loop(0, ITERS, one_step, 0)
    depth_out[...] = state[0, :rows, :cols]
    flow_x_out[...] = state[1, :rows, :cols]
    flow_y_out[...] = state[2, :rows, :cols]

    square = depths.shape
    onto = rows_of(square) == lanes_of(square)
    low = jnp.sum(jnp.where(onto, depths[...], 0.0), axis=0, keepdims=True)
    note = [low] + [jnp.zeros((1, 128), jnp.float32)] * (TILES - 1)
    for j in range(REACH):
        window = j + 1
        key = jnp.max(jnp.where(line_lane == known + 1 + window, low, -1.0), axis=1, keepdims=True)
        note[0] = jnp.where(line_lane == KEYS + j, key, note[0])
        lines = window_lines(saved, spots[j] // cols, lax.rem(spots[j], cols), window)
        for i, line in enumerate(lines):
            tile, at = PLACES[window, i]
            here = (line_lane >= at) & (line_lane < at + FIELDS * (2 * window + 1))
            note[tile] = jnp.where(here, turned(line, at, 1), note[tile])
    note = jnp.concatenate(note, axis=1)
    note_out[...] = jnp.broadcast_to(note[:, None, :], note_out.shape)


def per_device(depth, elevation, flow_x, flow_y, wet_mask, manning_class, manning_table):
    rough_sq = jnp.zeros(depth.shape, jnp.float32)
    for class_id in range(CLASSES):
        rough_sq = rough_sq + jnp.where(
            manning_class == class_id, manning_table[class_id] * manning_table[class_id], 0.0
        )
    wet_open = wet_mask.astype(jnp.float32)
    tile = depth.shape
    plane = ("core", "col")
    near_peers, far_peers = lax.axis_size("core") * lax.axis_size("col"), lax.axis_size("z")
    fields = with_halo(jnp.stack([depth, flow_x, flow_y, elevation, rough_sq, wet_open]))
    large = fields.shape[1:]

    def f32(*shape):
        return jax.ShapeDtypeStruct(shape, jnp.float32)

    merge = pl.pallas_call(merge_kernel, out_shape=f32(far_peers, 1, NOTE), name="merge_notes")

    def everywhere(note):
        over_plane = lax.all_to_all(note, plane, 0, 0, tiled=True)
        return lax.all_to_all(merge(over_plane), "z", 0, 0, tiled=True)

    def run(first, certain=False):
        vmem = pl.BlockSpec(memory_space=pltpu.VMEM)
        smem = pl.BlockSpec(memory_space=pltpu.SMEM)
        return pl.pallas_call(
            lambda *refs: run_kernel(tile, first, certain, *refs),
            in_specs=[vmem] if first else [vmem, vmem, smem, vmem],
            out_shape=(
                f32(*tile),
                f32(*tile),
                f32(*tile),
                f32(near_peers, 1, NOTE),
                f32(1, 128),
                jax.ShapeDtypeStruct((1,), jnp.int32),
            ),
            out_specs=(vmem, vmem, vmem, vmem, vmem, smem),
            scratch_shapes=[
                pltpu.VMEM((3, *large), jnp.float32),
                pltpu.VMEM((4, *large), jnp.float32),
                pltpu.VMEM((FIELDS, large[0] + 8, large[1]), jnp.float32),
                pltpu.VMEM((16, 128), jnp.float32),
                pltpu.VMEM((16, 128), jnp.float32),
                pltpu.SMEM((REACH,), jnp.int32),
            ],
            name="first_run" if first else "certain_run" if certain else "later_run",
        )

    def settled(notes, guess):
        true = jnp.max(notes[:, 0, :ITERS], axis=0)
        return jnp.all(true == guess[0, :ITERS])

    *result, note, guess, known = run(True)(fields)
    certain, later = run(False, True), run(False)
    for again in (certain, certain, later):
        *result, note, guess, known = again(everywhere(note), guess, known, fields)
    notes = everywhere(note)

    def unsettled(carry):
        return jnp.logical_not(carry[1]) & (carry[0] <= ITERS)

    def one_round(carry):
        count, _, notes, guess, known, _ = carry
        *result, note, guess, known = later(notes, guess, known, fields)
        notes = everywhere(note)
        return count + 1, settled(notes, guess), notes, guess, known, tuple(result)

    carry = (jnp.int32(0), settled(notes, guess), notes, guess, known, tuple(result))
    return lax.while_loop(unsettled, one_round, carry)[-1]


def solution(mesh):
    rows, cols = mesh.devices.shape
    split = jax.sharding.Mesh(mesh.devices.reshape(rows // 2, 2, cols), (*ROW, "col"))
    block = P(ROW, "col")
    return jax.shard_map(
        per_device,
        mesh=split,
        in_specs=(block, block, block, block, block, block, P()),
        out_specs=(block, block, block),
        check_vma=False,
    )
```

```python
import jax
import jax.numpy as jnp
from jax import lax
from jax.experimental import pallas as pl
from jax.experimental.pallas import tpu as pltpu
from jax.sharding import PartitionSpec as P

ITERS = 12
CLASSES = 8
HALO = ITERS

GRAVITY = 9.81
SPACING = 30.0
COURANT = 0.7
DRY_FLOOR = 0.01
FLOW_FLOOR = 0.05

ROW = ("z", "core")

REACH = 4
FIELDS = 6
KEYS = ITERS


def note_places():
    room = [ITERS + REACH]
    places = {}
    for window in range(REACH, 0, -1):
        span = FIELDS * (2 * window + 1)
        for row in range(window + 1):
            tile = next((t for t, used in enumerate(room) if used + span <= 128), len(room))
            if tile == len(room):
                room.append(0)
            places[window, row] = (tile, room[tile])
            room[tile] += span
    return places, len(room)


PLACES, TILES = note_places()
NOTE = 128 * TILES


def neighbours(axis):
    peers = lax.axis_size(axis)
    up = [(i, i + 1) for i in range(peers - 1)]
    down = [(j, i) for i, j in up]
    return up, down


def prepare_kernel(table, depth, elevation, flow_x, flow_y, wet, classes, fields, first, last, whole, sems):
    places = (
        (depth, fields.at[0]),
        (flow_x, fields.at[1]),
        (flow_y, fields.at[2]),
        (elevation, fields.at[3]),
        (classes, whole.at[0]),
        (wet, whole.at[1]),
    )
    copies = [pltpu.make_async_copy(src, dst, sems.at[i]) for i, (src, dst) in enumerate(places)]
    for copy in copies:
        copy.start()
    for copy in copies:
        copy.wait()
    class_of = whole[0]
    rough_sq = jnp.zeros(class_of.shape, jnp.float32)
    for class_id in range(CLASSES):
        rough_sq = rough_sq + jnp.where(class_of == class_id, table[class_id] * table[class_id], 0.0)
    fields[4] = rough_sq
    fields[5] = whole[1].astype(jnp.float32)
    rows = class_of.shape[0]
    for f in range(FIELDS):
        first[f] = fields[f, :HALO]
        last[f] = fields[f, rows - HALO :]


def edge_kernel(fields, after, before, tall, first, last):
    rows, cols = fields.shape[1:]
    shape = first.shape
    lane = lanes_of(shape)
    packed = [jnp.zeros(shape, jnp.float32)] * 2
    for f in range(FIELDS):
        tall[f, :rows] = fields[f]
        tall[f, rows : rows + HALO] = after[f]
        tall[f, rows + HALO :] = before[f]
        here = (lane >= HALO * f) & (lane < HALO * (f + 1))
        whole = tall[f]
        for end, start in enumerate((0, cols - HALO)):
            packed[end] = jnp.where(here, turned(whole, HALO * f - start, 1), packed[end])
    first[...] = packed[0]
    last[...] = packed[1]


def join(fields, tall, after, before):
    cols = tall.shape[2]
    lane = lanes_of(after.shape)
    ahead, behind = after[...], before[...]
    for f in range(FIELDS):
        fields[f, :, :cols] = tall[f]
        rest = jnp.where(lane < HALO, turned(ahead, -HALO * f, 1), 0.0)
        rest = jnp.where(lane >= cols - HALO, turned(behind, cols - HALO - HALO * f, 1), rest)
        fields[f, :, cols:] = rest


def next_of(x, axis):
    return pltpu.roll(x, x.shape[axis] - 1, axis)


def previous_of(x, axis):
    return pltpu.roll(x, 1, axis)


def step_of(deepest):
    return COURANT * SPACING / jnp.sqrt(GRAVITY * jnp.maximum(deepest, DRY_FLOOR))


def fixed_parts(bed, opening):
    return tuple(
        (jnp.maximum(bed, next_of(bed, axis)), opening * next_of(opening, axis)) for axis in (0, 1)
    )


def face_flux(flow_old, surface, surf_high, bed_max, rough, opening, time_step):
    flow_depth = jnp.maximum(surface, surf_high) - bed_max
    driving = jnp.maximum(flow_depth, 0.0)
    friction_depth = jnp.maximum(flow_depth, FLOW_FLOOR)
    slope = (surf_high - surface) / SPACING
    driven = flow_old - GRAVITY * driving * time_step * slope
    damping = 1.0 + GRAVITY * time_step * rough * jnp.abs(flow_old) * jnp.exp(
        -7.0 / 3.0 * jnp.log(friction_depth)
    )
    return opening * driven / damping


def advance(depth, flow_x, flow_y, bed, rough, faces, time_step):
    surface = depth + bed
    (bed_x, open_x), (bed_y, open_y) = faces
    rows_new = face_flux(flow_x, surface, next_of(surface, 0), bed_x, rough, open_x, time_step)
    cols_new = face_flux(flow_y, surface, next_of(surface, 1), bed_y, rough, open_y, time_step)
    change = previous_of(rows_new, 0) - rows_new + (previous_of(cols_new, 1) - cols_new)
    return jnp.maximum(depth + time_step / SPACING * change, 0.0), rows_new, cols_new


def lanes_of(shape):
    return lax.broadcasted_iota(jnp.int32, shape, len(shape) - 1)


def rows_of(shape):
    return lax.broadcasted_iota(jnp.int32, shape, len(shape) - 2)


def total(x, how):
    return how(how(x, axis=0, keepdims=True), axis=1, keepdims=True)


def merged(notes):
    head = notes[:, :128]
    lane = lanes_of(head.shape)
    out_lane = lanes_of((1, NOTE))
    place = rows_of((notes.shape[0], 1)).astype(jnp.float32)
    out = jnp.max(notes, axis=0, keepdims=True)
    for window in range(1, REACH + 1):
        keyed = jnp.max(jnp.where(lane == KEYS + window - 1, head, -1.0), axis=1, keepdims=True)
        best = keyed == jnp.max(keyed, axis=0, keepdims=True)
        first = jnp.min(jnp.where(best, place, 1e6), axis=0, keepdims=True)
        chosen = jnp.sum(jnp.where(place == first, notes, 0.0), axis=0, keepdims=True)
        for row in range(window + 1):
            tile, at = PLACES[window, row]
            start = 128 * tile + at
            here = (out_lane >= start) & (out_lane < start + FIELDS * (2 * window + 1))
            out = jnp.where(here, chosen, out)
    return out


def merge_kernel(notes, out):
    out[...] = jnp.broadcast_to(merged(notes[:, 0, :])[:, None, :], out.shape)


def turned(x, shift, axis):
    size = x.shape[axis]
    return pltpu.roll(x, shift % size, axis) if shift % size else x


def window_shape(window):
    return (8 if 2 * window < 8 else 16, 128)


def columns_of(shape, width):
    lane = lanes_of(shape)
    column = lane
    for f in range(1, FIELDS):
        column = jnp.where(lane >= width * f, lane - width * f, column)
    return column


def window_fields(note, window):
    width = 2 * window + 1
    shape = window_shape(window)
    row, lane = rows_of(shape), lanes_of(shape)
    column = columns_of(shape, width)
    folded = jnp.zeros(shape, jnp.float32)
    for i in range(window + 1):
        tile, at = PLACES[window, i]
        line = turned(note[:, 128 * tile : 128 * (tile + 1)], -at, 1)
        folded = jnp.where(row == i, jnp.broadcast_to(line, shape), folded)
    lower = turned(folded, window + 1, 0)
    lower = jnp.where(column <= window, turned(lower, -window, 1), turned(lower, window + 1, 1))
    packed = jnp.where(row <= window, folded, lower)
    inside = jnp.abs(column - window) + jnp.abs(row - window) <= window
    packed = jnp.where(inside, packed, 0.0)
    return [jnp.where(lane < width, turned(packed, -width * f, 1), 0.0) for f in range(FIELDS)]


def window_lines(saved, at_row, at_col, window):
    width = 2 * window + 1
    shape = window_shape(window)
    row, lane = rows_of(shape), lanes_of(shape)
    column = columns_of(shape, width)
    packed = jnp.zeros(shape, jnp.float32)
    top = at_row + 8 - window
    off = lax.rem(top, 8)
    height = shape[0] + 8
    for f in range(FIELDS):
        strip = saved[f, pl.ds(pl.multiple_of(top - off, 8), height), :]
        strip = pltpu.roll(strip, lax.rem(height - off, height), 0)[: shape[0]]
        shift = lax.rem(width * f + window - at_col + 2 * 256, 256)
        moved = pltpu.roll(strip, shift, 1)[:, :128]
        packed = jnp.where((lane >= width * f) & (lane < width * (f + 1)), moved, packed)
    lower = turned(packed, -(window + 1), 0)
    lower = jnp.where(column > window, turned(lower, window, 1), turned(lower, -(window + 1), 1))
    folded = jnp.where(jnp.abs(column - window) <= row, packed, lower)
    return [folded[i : i + 1] for i in range(window + 1)]


def run_kernel(tile, first, certain, *refs):
    if first:
        tall, after, before, fields, depth_out, flow_x_out, flow_y_out, note_out, guess_out, known_out = refs[:10]
        join(fields, tall, after, before)
    else:
        notes, guess_in, known_in, fields, depth_out, flow_x_out, flow_y_out, note_out, guess_out, known_out = refs[:10]
    state, faces, saved, guesses, depths, spots = refs[-6:]
    rows, cols = tile
    line_lane = lanes_of((1, 128))

    if first:
        known = jnp.int32(-1)
        guess_out[...] = jnp.full((1, 128), -1.0, jnp.float32)
    else:
        note = merged(notes[:, 0, :])
        true = note[:, :128]
        old = guess_in[...]
        wrong = jnp.where((true != old) & (line_lane < ITERS), line_lane.astype(jnp.float32), 1.0 * ITERS)
        miss = jnp.min(wrong).astype(jnp.int32)
        before = known_in[0]
        held = miss > before
        guess = true
        windows = {w: window_fields(note, w) for w in range(1, REACH + 1)}
        walls = {w: fixed_parts(parts[3], parts[5]) for w, parts in windows.items()}
        moving = {w: parts[:3] for w, parts in windows.items()}
        for stage in range(1, REACH + 1):
            level = jnp.max(jnp.where(line_lane == before + stage, guess, 0.0), axis=1, keepdims=True)
            time_step = step_of(level)
            for w in range(stage, REACH + 1):
                moving[w] = advance(*moving[w], windows[w][3], windows[w][4], walls[w], time_step)
            shape = window_shape(stage)
            here = (rows_of(shape) == stage) & (lanes_of(shape) == stage)
            centre = total(jnp.where(here, moving[stage][0], 0.0), jnp.max)
            target = before + stage + 1
            use = held & (target > miss) & (line_lane == target) & (centre > 0.0)
            guess = jnp.where(use, centre, guess)
        known = miss
        if not certain:
            known = jnp.where(held, jnp.maximum(before + REACH + 1, miss), miss)
        guess_out[...] = guess
        square = (16, 128)
        onto = rows_of(square) == lanes_of(square)
        spread = jnp.sum(jnp.where(onto, jnp.broadcast_to(guess, square), 0.0), axis=1, keepdims=True)
        guesses[...] = jnp.broadcast_to(spread, square)
    known_out[0] = known

    for f in range(3):
        state[f] = fields[f]
    bed, rough, opening = fields[3], fields[4], fields[5]
    for axis, (bed_max, both) in enumerate(fixed_parts(bed, opening)):
        faces[2 * axis] = bed_max
        faces[2 * axis + 1] = both
    last = fields.shape[1] - 8
    for f in range(3, FIELDS):
        saved[f, :8] = fields[f, last:]
        saved[f, 8:] = fields[f]
    depths[...] = jnp.full(depths.shape, -1.0, jnp.float32)

    def one_step(step, carry):
        depth, flow_x, flow_y = state[0], state[1], state[2]
        own = depth[:rows, :cols]
        deepest = total(own, jnp.max)
        depths[pl.ds(step, 1), :] = jnp.broadcast_to(deepest, (1, 128))

        @pl.when(step == known + 1)
        def _():
            for f in range(3):
                saved[f, :8] = state[f, last:]
                saved[f, 8:] = state[f]

        for j in range(REACH):

            @pl.when(step == known + 2 + j)
            def _():
                cell = (rows_of((rows, cols)) * cols + lanes_of((rows, cols))).astype(jnp.float32)
                spots[j] = jnp.min(jnp.where(own == deepest, cell, 1.0 * (rows * cols - 1))).astype(jnp.int32)

        level = deepest if first else guesses[pl.ds(step, 1), :][:, :1]
        new = advance(
            depth,
            flow_x,
            flow_y,
            fields[3],
            fields[4],
            ((faces[0], faces[1]), (faces[2], faces[3])),
            step_of(level),
        )
        for f in range(3):
            state[f] = new[f]
        return carry

    for j in range(REACH):
        spots[j] = 0
    lax.fori_loop(0, ITERS, one_step, 0)
    depth_out[...] = state[0, :rows, :cols]
    flow_x_out[...] = state[1, :rows, :cols]
    flow_y_out[...] = state[2, :rows, :cols]

    square = depths.shape
    onto = rows_of(square) == lanes_of(square)
    low = jnp.sum(jnp.where(onto, depths[...], 0.0), axis=0, keepdims=True)
    note = [low] + [jnp.zeros((1, 128), jnp.float32)] * (TILES - 1)
    for j in range(REACH):
        window = j + 1
        key = jnp.max(jnp.where(line_lane == known + 1 + window, low, -1.0), axis=1, keepdims=True)
        note[0] = jnp.where(line_lane == KEYS + j, key, note[0])
        lines = window_lines(saved, spots[j] // cols, lax.rem(spots[j], cols), window)
        for i, line in enumerate(lines):
            tile, at = PLACES[window, i]
            here = (line_lane >= at) & (line_lane < at + FIELDS * (2 * window + 1))
            note[tile] = jnp.where(here, turned(line, at, 1), note[tile])
    note = jnp.concatenate(note, axis=1)
    note_out[...] = jnp.broadcast_to(note[:, None, :], note_out.shape)


def per_device(depth, elevation, flow_x, flow_y, wet_mask, manning_class, manning_table):
    tile = depth.shape
    plane = ("core", "col")
    near_peers, far_peers = lax.axis_size("core") * lax.axis_size("col"), lax.axis_size("z")
    rows, cols = tile
    large = (rows + 2 * HALO, 2 * cols)
    vmem = pl.BlockSpec(memory_space=pltpu.VMEM)
    smem = pl.BlockSpec(memory_space=pltpu.SMEM)

    def f32(*shape):
        return jax.ShapeDtypeStruct(shape, jnp.float32)

    fields, first, last = pl.pallas_call(
        prepare_kernel,
        in_specs=[smem] + [pl.BlockSpec(memory_space=pl.ANY)] * 6,
        out_shape=(f32(FIELDS, *tile), f32(FIELDS, HALO, cols), f32(FIELDS, HALO, cols)),
        out_specs=(vmem,) * 3,
        scratch_shapes=[pltpu.VMEM((2, *tile), jnp.int32), pltpu.SemaphoreType.DMA((6,))],
        name="prepare",
    )(manning_table, depth, elevation, flow_x, flow_y, wet_mask, manning_class)
    up, down = neighbours(ROW)
    before, after = lax.ppermute(last, ROW, up), lax.ppermute(first, ROW, down)
    tall, first, last = pl.pallas_call(
        edge_kernel,
        in_specs=[vmem] * 3,
        out_shape=(f32(FIELDS, large[0], cols), f32(large[0], 128), f32(large[0], 128)),
        out_specs=(vmem,) * 3,
        name="edges",
    )(fields, after, before)
    up, down = neighbours("col")
    before, after = lax.ppermute(last, "col", up), lax.ppermute(first, "col", down)

    merge = pl.pallas_call(merge_kernel, out_shape=f32(far_peers, 1, NOTE), name="merge_notes")

    def everywhere(note):
        over_plane = lax.all_to_all(note, plane, 0, 0, tiled=True)
        return lax.all_to_all(merge(over_plane), "z", 0, 0, tiled=True)

    def run(first, certain=False):
        whole = (f32(FIELDS, *large),) if first else ()
        return pl.pallas_call(
            lambda *refs: run_kernel(tile, first, certain, *refs),
            in_specs=[vmem] * 3 if first else [vmem, vmem, smem, vmem],
            out_shape=(
                *whole,
                f32(*tile),
                f32(*tile),
                f32(*tile),
                f32(near_peers, 1, NOTE),
                f32(1, 128),
                jax.ShapeDtypeStruct((1,), jnp.int32),
            ),
            out_specs=(vmem,) * (5 + len(whole)) + (smem,),
            scratch_shapes=[
                pltpu.VMEM((3, *large), jnp.float32),
                pltpu.VMEM((4, *large), jnp.float32),
                pltpu.VMEM((FIELDS, large[0] + 8, large[1]), jnp.float32),
                pltpu.VMEM((16, 128), jnp.float32),
                pltpu.VMEM((16, 128), jnp.float32),
                pltpu.SMEM((REACH,), jnp.int32),
            ],
            name="first_run" if first else "certain_run" if certain else "later_run",
        )

    def settled(notes, guess):
        true = jnp.max(notes[:, 0, :ITERS], axis=0)
        return jnp.all(true == guess[0, :ITERS])

    fields, *result, note, guess, known = run(True)(tall, after, before)
    certain, later = run(False, True), run(False)
    for again in (certain, certain, later):
        *result, note, guess, known = again(everywhere(note), guess, known, fields)
    notes = everywhere(note)

    def unsettled(carry):
        return jnp.logical_not(carry[1]) & (carry[0] <= ITERS)

    def one_round(carry):
        count, _, notes, guess, known, _ = carry
        *result, note, guess, known = later(notes, guess, known, fields)
        notes = everywhere(note)
        return count + 1, settled(notes, guess), notes, guess, known, tuple(result)

    carry = (jnp.int32(0), settled(notes, guess), notes, guess, known, tuple(result))
    return lax.while_loop(unsettled, one_round, carry)[-1]


def solution(mesh):
    rows, cols = mesh.devices.shape
    split = jax.sharding.Mesh(mesh.devices.reshape(rows // 2, 2, cols), (*ROW, "col"))
    block = P(ROW, "col")
    return jax.shard_map(
        per_device,
        mesh=split,
        in_specs=(block, block, block, block, block, block, P()),
        out_specs=(block, block, block),
        check_vma=False,
    )
```

```python
import jax
import jax.numpy as jnp
from jax import lax
from jax.experimental import pallas as pl
from jax.experimental.pallas import tpu as pltpu
from jax.sharding import PartitionSpec as P

ITERS = 12
CLASSES = 8
HALO = ITERS

GRAVITY = 9.81
SPACING = 30.0
COURANT = 0.7
DRY_FLOOR = 0.01
FLOW_FLOOR = 0.05

ROW = ("z", "core")

REACH = 4
FIELDS = 6
KEYS = ITERS


def note_places():
    room = [ITERS + REACH]
    places = {}
    for window in range(REACH, 0, -1):
        span = FIELDS * (2 * window + 1)
        for row in range(window + 1):
            tile = next((t for t, used in enumerate(room) if used + span <= 128), len(room))
            if tile == len(room):
                room.append(0)
            places[window, row] = (tile, room[tile])
            room[tile] += span
    return places, len(room)


PLACES, TILES = note_places()
NOTE = 128 * TILES
BRIEF = 128
UNUSED = 1000


def neighbours(axis):
    peers = lax.axis_size(axis)
    up = [(i, i + 1) for i in range(peers - 1)]
    down = [(j, i) for i, j in up]
    return up, down


def prepare_kernel(table, depth, elevation, flow_x, flow_y, wet, classes, fields, first, last, whole, sems):
    places = (
        (depth, fields.at[0]),
        (flow_x, fields.at[1]),
        (flow_y, fields.at[2]),
        (elevation, fields.at[3]),
        (classes, whole.at[0]),
        (wet, whole.at[1]),
    )
    copies = [pltpu.make_async_copy(src, dst, sems.at[i]) for i, (src, dst) in enumerate(places)]
    for copy in copies:
        copy.start()
    for copy in copies:
        copy.wait()
    class_of = whole[0]
    rough_sq = jnp.zeros(class_of.shape, jnp.float32)
    for class_id in range(CLASSES):
        rough_sq = rough_sq + jnp.where(class_of == class_id, table[class_id] * table[class_id], 0.0)
    fields[4] = rough_sq
    fields[5] = whole[1].astype(jnp.float32)
    rows = class_of.shape[0]
    for f in range(FIELDS):
        first[f] = fields[f, :HALO]
        last[f] = fields[f, rows - HALO :]


def edge_kernel(fields, after, before, tall, first, last):
    rows, cols = fields.shape[1:]
    shape = first.shape
    lane = lanes_of(shape)
    packed = [jnp.zeros(shape, jnp.float32)] * 2
    for f in range(FIELDS):
        tall[f, :rows] = fields[f]
        tall[f, rows : rows + HALO] = after[f]
        tall[f, rows + HALO :] = before[f]
        here = (lane >= HALO * f) & (lane < HALO * (f + 1))
        whole = tall[f]
        for end, start in enumerate((0, cols - HALO)):
            packed[end] = jnp.where(here, turned(whole, HALO * f - start, 1), packed[end])
    first[...] = packed[0]
    last[...] = packed[1]


def join(fields, tall, after, before):
    cols = tall.shape[2]
    lane = lanes_of(after.shape)
    ahead, behind = after[...], before[...]
    for f in range(FIELDS):
        fields[f, :, :cols] = tall[f]
        rest = jnp.where(lane < HALO, turned(ahead, -HALO * f, 1), 0.0)
        rest = jnp.where(lane >= cols - HALO, turned(behind, cols - HALO - HALO * f, 1), rest)
        fields[f, :, cols:] = rest


def next_of(x, axis):
    return pltpu.roll(x, x.shape[axis] - 1, axis)


def previous_of(x, axis):
    return pltpu.roll(x, 1, axis)


def step_of(deepest):
    return COURANT * SPACING / jnp.sqrt(GRAVITY * jnp.maximum(deepest, DRY_FLOOR))


def fixed_parts(bed, opening):
    return tuple(
        (jnp.maximum(bed, next_of(bed, axis)), opening * next_of(opening, axis)) for axis in (0, 1)
    )


def face_flux(flow_old, surface, surf_high, bed_max, rough, opening, time_step):
    flow_depth = jnp.maximum(surface, surf_high) - bed_max
    driving = jnp.maximum(flow_depth, 0.0)
    friction_depth = jnp.maximum(flow_depth, FLOW_FLOOR)
    slope = (surf_high - surface) / SPACING
    driven = flow_old - GRAVITY * driving * time_step * slope
    damping = 1.0 + GRAVITY * time_step * rough * jnp.abs(flow_old) * jnp.exp(
        -7.0 / 3.0 * jnp.log(friction_depth)
    )
    return opening * driven / damping


def advance(depth, flow_x, flow_y, bed, rough, faces, time_step):
    surface = depth + bed
    (bed_x, open_x), (bed_y, open_y) = faces
    rows_new = face_flux(flow_x, surface, next_of(surface, 0), bed_x, rough, open_x, time_step)
    cols_new = face_flux(flow_y, surface, next_of(surface, 1), bed_y, rough, open_y, time_step)
    change = previous_of(rows_new, 0) - rows_new + (previous_of(cols_new, 1) - cols_new)
    return jnp.maximum(depth + time_step / SPACING * change, 0.0), rows_new, cols_new


def lanes_of(shape):
    return lax.broadcasted_iota(jnp.int32, shape, len(shape) - 1)


def rows_of(shape):
    return lax.broadcasted_iota(jnp.int32, shape, len(shape) - 2)


def total(x, how):
    return how(how(x, axis=0, keepdims=True), axis=1, keepdims=True)


def merged(notes):
    if notes.shape[1] == BRIEF:
        return jnp.max(notes, axis=0, keepdims=True)
    head = notes[:, :128]
    lane = lanes_of(head.shape)
    out_lane = lanes_of((1, NOTE))
    place = rows_of((notes.shape[0], 1)).astype(jnp.float32)
    out = jnp.max(notes, axis=0, keepdims=True)
    for window in range(1, REACH + 1):
        keyed = jnp.max(jnp.where(lane == KEYS + window - 1, head, -1.0), axis=1, keepdims=True)
        best = keyed == jnp.max(keyed, axis=0, keepdims=True)
        first = jnp.min(jnp.where(best, place, 1e6), axis=0, keepdims=True)
        chosen = jnp.sum(jnp.where(place == first, notes, 0.0), axis=0, keepdims=True)
        for row in range(window + 1):
            tile, at = PLACES[window, row]
            start = 128 * tile + at
            here = (out_lane >= start) & (out_lane < start + FIELDS * (2 * window + 1))
            out = jnp.where(here, chosen, out)
    return out


def merge_kernel(notes, out):
    out[...] = jnp.broadcast_to(merged(notes[:, 0, :])[:, None, :], out.shape)


def turned(x, shift, axis):
    size = x.shape[axis]
    return pltpu.roll(x, shift % size, axis) if shift % size else x


def window_shape(window):
    return (8 if 2 * window < 8 else 16, 128)


def columns_of(shape, width):
    lane = lanes_of(shape)
    column = lane
    for f in range(1, FIELDS):
        column = jnp.where(lane >= width * f, lane - width * f, column)
    return column


def window_fields(note, window):
    width = 2 * window + 1
    shape = window_shape(window)
    row, lane = rows_of(shape), lanes_of(shape)
    column = columns_of(shape, width)
    folded = jnp.zeros(shape, jnp.float32)
    for i in range(window + 1):
        tile, at = PLACES[window, i]
        line = turned(note[:, 128 * tile : 128 * (tile + 1)], -at, 1)
        folded = jnp.where(row == i, jnp.broadcast_to(line, shape), folded)
    lower = turned(folded, window + 1, 0)
    lower = jnp.where(column <= window, turned(lower, -window, 1), turned(lower, window + 1, 1))
    packed = jnp.where(row <= window, folded, lower)
    inside = jnp.abs(column - window) + jnp.abs(row - window) <= window
    packed = jnp.where(inside, packed, 0.0)
    return [jnp.where(lane < width, turned(packed, -width * f, 1), 0.0) for f in range(FIELDS)]


def window_lines(saved, at_row, at_col, window):
    width = 2 * window + 1
    shape = window_shape(window)
    row, lane = rows_of(shape), lanes_of(shape)
    column = columns_of(shape, width)
    packed = jnp.zeros(shape, jnp.float32)
    top = at_row + 8 - window
    off = lax.rem(top, 8)
    height = shape[0] + 8
    for f in range(FIELDS):
        strip = saved[f, pl.ds(pl.multiple_of(top - off, 8), height), :]
        strip = pltpu.roll(strip, lax.rem(height - off, height), 0)[: shape[0]]
        shift = lax.rem(width * f + window - at_col + 2 * 256, 256)
        moved = pltpu.roll(strip, shift, 1)[:, :128]
        packed = jnp.where((lane >= width * f) & (lane < width * (f + 1)), moved, packed)
    lower = turned(packed, -(window + 1), 0)
    lower = jnp.where(column > window, turned(lower, window, 1), turned(lower, -(window + 1), 1))
    folded = jnp.where(jnp.abs(column - window) <= row, packed, lower)
    return [folded[i : i + 1] for i in range(window + 1)]


def run_kernel(tile, first, certain, reads, writes, *refs):
    if first:
        tall, after, before, fields, depth_out, flow_x_out, flow_y_out, note_out, guess_out, known_out = refs[:10]
        join(fields, tall, after, before)
    else:
        notes, guess_in, known_in, fields, depth_out, flow_x_out, flow_y_out, note_out, guess_out, known_out = refs[:10]
    state, faces, saved, guesses, depths, spots = refs[-6:]
    rows, cols = tile
    line_lane = lanes_of((1, 128))

    if first:
        known = jnp.int32(-1)
        guess_out[...] = jnp.full((1, 128), -1.0, jnp.float32)
    else:
        note = merged(notes[:, 0, :])
        true = note[:, :128]
        old = guess_in[...]
        wrong = jnp.where((true != old) & (line_lane < ITERS), line_lane.astype(jnp.float32), 1.0 * ITERS)
        miss = jnp.min(wrong).astype(jnp.int32)
        before = known_in[0]
        held = miss > before
        guess = true
        if reads:
            windows = {w: window_fields(note, w) for w in range(1, REACH + 1)}
            walls = {w: fixed_parts(parts[3], parts[5]) for w, parts in windows.items()}
            moving = {w: parts[:3] for w, parts in windows.items()}
            for stage in range(1, REACH + 1):
                level = jnp.max(jnp.where(line_lane == before + stage, guess, 0.0), axis=1, keepdims=True)
                time_step = step_of(level)
                for w in range(stage, REACH + 1):
                    moving[w] = advance(*moving[w], windows[w][3], windows[w][4], walls[w], time_step)
                shape = window_shape(stage)
                here = (rows_of(shape) == stage) & (lanes_of(shape) == stage)
                centre = total(jnp.where(here, moving[stage][0], 0.0), jnp.max)
                target = before + stage + 1
                use = held & (target > miss) & (line_lane == target) & (centre > 0.0)
                guess = jnp.where(use, centre, guess)
        known = miss
        if reads and not certain:
            known = jnp.where(held, jnp.maximum(before + REACH + 1, miss), miss)
        guess_out[...] = guess
        square = (16, 128)
        onto = rows_of(square) == lanes_of(square)
        spread = jnp.sum(jnp.where(onto, jnp.broadcast_to(guess, square), 0.0), axis=1, keepdims=True)
        guesses[...] = jnp.broadcast_to(spread, square)
    known_out[0] = known if writes or first else jnp.int32(UNUSED)

    for f in range(3):
        state[f] = fields[f]
    bed, rough, opening = fields[3], fields[4], fields[5]
    for axis, (bed_max, both) in enumerate(fixed_parts(bed, opening)):
        faces[2 * axis] = bed_max
        faces[2 * axis + 1] = both
    last = fields.shape[1] - 8
    if writes:
        for f in range(3, FIELDS):
            saved[f, :8] = fields[f, last:]
            saved[f, 8:] = fields[f]
    depths[...] = jnp.full(depths.shape, -1.0, jnp.float32)

    def one_step(step, carry):
        depth, flow_x, flow_y = state[0], state[1], state[2]
        own = depth[:rows, :cols]
        deepest = total(own, jnp.max)
        depths[pl.ds(step, 1), :] = jnp.broadcast_to(deepest, (1, 128))

        @pl.when((step == known + 1) & writes)
        def _():
            for f in range(3):
                saved[f, :8] = state[f, last:]
                saved[f, 8:] = state[f]

        for j in range(REACH if writes else 0):

            @pl.when(step == known + 2 + j)
            def _():
                cell = (rows_of((rows, cols)) * cols + lanes_of((rows, cols))).astype(jnp.float32)
                spots[j] = jnp.min(jnp.where(own == deepest, cell, 1.0 * (rows * cols - 1))).astype(jnp.int32)

        level = deepest if first else guesses[pl.ds(step, 1), :][:, :1]
        new = advance(
            depth,
            flow_x,
            flow_y,
            fields[3],
            fields[4],
            ((faces[0], faces[1]), (faces[2], faces[3])),
            step_of(level),
        )
        for f in range(3):
            state[f] = new[f]
        return carry

    for j in range(REACH):
        spots[j] = 0
    lax.fori_loop(0, ITERS, one_step, 0)
    depth_out[...] = state[0, :rows, :cols]
    flow_x_out[...] = state[1, :rows, :cols]
    flow_y_out[...] = state[2, :rows, :cols]

    square = depths.shape
    onto = rows_of(square) == lanes_of(square)
    low = jnp.sum(jnp.where(onto, depths[...], 0.0), axis=0, keepdims=True)
    note = [low] + [jnp.zeros((1, 128), jnp.float32)] * (TILES - 1 if writes else 0)
    for j in range(REACH if writes else 0):
        window = j + 1
        key = jnp.max(jnp.where(line_lane == known + 1 + window, low, -1.0), axis=1, keepdims=True)
        note[0] = jnp.where(line_lane == KEYS + j, key, note[0])
        lines = window_lines(saved, spots[j] // cols, lax.rem(spots[j], cols), window)
        for i, line in enumerate(lines):
            tile, at = PLACES[window, i]
            here = (line_lane >= at) & (line_lane < at + FIELDS * (2 * window + 1))
            note[tile] = jnp.where(here, turned(line, at, 1), note[tile])
    note = jnp.concatenate(note, axis=1) if writes else low
    note_out[...] = jnp.broadcast_to(note[:, None, :], note_out.shape)


def per_device(depth, elevation, flow_x, flow_y, wet_mask, manning_class, manning_table):
    tile = depth.shape
    plane = ("core", "col")
    near_peers, far_peers = lax.axis_size("core") * lax.axis_size("col"), lax.axis_size("z")
    rows, cols = tile
    large = (rows + 2 * HALO, 2 * cols)
    vmem = pl.BlockSpec(memory_space=pltpu.VMEM)
    smem = pl.BlockSpec(memory_space=pltpu.SMEM)

    def f32(*shape):
        return jax.ShapeDtypeStruct(shape, jnp.float32)

    fields, first, last = pl.pallas_call(
        prepare_kernel,
        in_specs=[smem] + [pl.BlockSpec(memory_space=pl.ANY)] * 6,
        out_shape=(f32(FIELDS, *tile), f32(FIELDS, HALO, cols), f32(FIELDS, HALO, cols)),
        out_specs=(vmem,) * 3,
        scratch_shapes=[pltpu.VMEM((2, *tile), jnp.int32), pltpu.SemaphoreType.DMA((6,))],
        name="prepare",
    )(manning_table, depth, elevation, flow_x, flow_y, wet_mask, manning_class)
    up, down = neighbours(ROW)
    before, after = lax.ppermute(last, ROW, up), lax.ppermute(first, ROW, down)
    tall, first, last = pl.pallas_call(
        edge_kernel,
        in_specs=[vmem] * 3,
        out_shape=(f32(FIELDS, large[0], cols), f32(large[0], 128), f32(large[0], 128)),
        out_specs=(vmem,) * 3,
        name="edges",
    )(fields, after, before)
    up, down = neighbours("col")
    before, after = lax.ppermute(last, "col", up), lax.ppermute(first, "col", down)

    def everywhere(note):
        over_plane = lax.all_to_all(note, plane, 0, 0, tiled=True)
        merge = pl.pallas_call(merge_kernel, out_shape=f32(far_peers, 1, note.shape[2]), name="merge_notes")
        return lax.all_to_all(merge(over_plane), "z", 0, 0, tiled=True)

    def run(name, certain=False, reads=True, writes=True):
        first = name == "first_run"
        whole = (f32(FIELDS, *large),) if first else ()
        return pl.pallas_call(
            lambda *refs: run_kernel(tile, first, certain, reads, writes, *refs),
            in_specs=[vmem] * 3 if first else [vmem, vmem, smem, vmem],
            out_shape=(
                *whole,
                f32(*tile),
                f32(*tile),
                f32(*tile),
                f32(near_peers, 1, NOTE if writes else BRIEF),
                f32(1, 128),
                jax.ShapeDtypeStruct((1,), jnp.int32),
            ),
            out_specs=(vmem,) * (5 + len(whole)) + (smem,),
            scratch_shapes=[
                pltpu.VMEM((3, *large), jnp.float32),
                pltpu.VMEM((4, *large), jnp.float32),
                pltpu.VMEM((FIELDS, large[0] + 8, large[1]), jnp.float32),
                pltpu.VMEM((16, 128), jnp.float32),
                pltpu.VMEM((16, 128), jnp.float32),
                pltpu.SMEM((REACH,), jnp.int32),
            ],
            name=name,
        )

    def settled(notes, guess):
        true = jnp.max(notes[:, 0, :ITERS], axis=0)
        return jnp.all(true == guess[0, :ITERS])

    fields, *result, note, guess, known = run("first_run", reads=False, writes=False)(tall, after, before)
    later = run("later_run")
    for again in (
        run("second_run", certain=True, reads=False),
        run("third_run", certain=True),
        later,
        run("check_run", writes=False),
    ):
        *result, note, guess, known = again(everywhere(note), guess, known, fields)
    notes = everywhere(note)
    done = settled(notes, guess)
    notes = jnp.pad(notes, ((0, 0), (0, 0), (0, NOTE - BRIEF)))

    def unsettled(carry):
        return jnp.logical_not(carry[1]) & (carry[0] <= ITERS)

    def one_round(carry):
        count, _, notes, guess, known, _ = carry
        *result, note, guess, known = later(notes, guess, known, fields)
        notes = everywhere(note)
        return count + 1, settled(notes, guess), notes, guess, known, tuple(result)

    carry = (jnp.int32(0), done, notes, guess, known, tuple(result))
    return lax.while_loop(unsettled, one_round, carry)[-1]


def solution(mesh):
    rows, cols = mesh.devices.shape
    split = jax.sharding.Mesh(mesh.devices.reshape(rows // 2, 2, cols), (*ROW, "col"))
    block = P(ROW, "col")
    return jax.shard_map(
        per_device,
        mesh=split,
        in_specs=(block, block, block, block, block, block, P()),
        out_specs=(block, block, block),
        check_vma=False,
    )
```

```python
import jax
import jax.numpy as jnp
from jax import lax
from jax.experimental import pallas as pl
from jax.experimental.pallas import tpu as pltpu
from jax.sharding import PartitionSpec as P

ITERS = 12
CLASSES = 8
HALO = ITERS

GRAVITY = 9.81
SPACING = 30.0
COURANT = 0.7
DRY_FLOOR = 0.01
FLOW_FLOOR = 0.05

ROW = ("z", "core")

REACH = 4
FIELDS = 6
KEYS = ITERS


def note_places():
    room = [ITERS + REACH]
    places = {}
    for window in range(REACH, 0, -1):
        span = FIELDS * (2 * window + 1)
        for row in range(window + 1):
            tile = next((t for t, used in enumerate(room) if used + span <= 128), len(room))
            if tile == len(room):
                room.append(0)
            places[window, row] = (tile, room[tile])
            room[tile] += span
    return places, len(room)


PLACES, TILES = note_places()
NOTE = 128 * TILES
BRIEF = 128
UNUSED = 1000


def neighbours(axis):
    peers = lax.axis_size(axis)
    up = [(i, i + 1) for i in range(peers - 1)]
    down = [(j, i) for i, j in up]
    return up, down


def prepare_kernel(table, depth, elevation, flow_x, flow_y, wet, classes, fields, first, last, whole, sems):
    places = (
        (depth, fields.at[0]),
        (flow_x, fields.at[1]),
        (flow_y, fields.at[2]),
        (elevation, fields.at[3]),
        (classes, whole.at[0]),
        (wet, whole.at[1]),
    )
    copies = [pltpu.make_async_copy(src, dst, sems.at[i]) for i, (src, dst) in enumerate(places)]
    for copy in copies:
        copy.start()
    for copy in copies:
        copy.wait()
    class_of = whole[0]
    rough_sq = jnp.zeros(class_of.shape, jnp.float32)
    for class_id in range(CLASSES):
        rough_sq = rough_sq + jnp.where(class_of == class_id, table[class_id] * table[class_id], 0.0)
    fields[4] = rough_sq
    fields[5] = whole[1].astype(jnp.float32)
    rows = class_of.shape[0]
    for f in range(FIELDS):
        first[f] = fields[f, :HALO]
        last[f] = fields[f, rows - HALO :]


def edge_kernel(fields, after, before, tall, first, last):
    rows, cols = fields.shape[1:]
    shape = first.shape
    lane = lanes_of(shape)
    packed = [jnp.zeros(shape, jnp.float32)] * 2
    for f in range(FIELDS):
        tall[f, :rows] = fields[f]
        tall[f, rows : rows + HALO] = after[f]
        tall[f, rows + HALO :] = before[f]
        here = (lane >= HALO * f) & (lane < HALO * (f + 1))
        whole = tall[f]
        for end, start in enumerate((0, cols - HALO)):
            packed[end] = jnp.where(here, turned(whole, HALO * f - start, 1), packed[end])
    first[...] = packed[0]
    last[...] = packed[1]


def join(fields, tall, after, before):
    cols = tall.shape[2]
    lane = lanes_of(after.shape)
    ahead, behind = after[...], before[...]
    for f in range(FIELDS):
        fields[f, :, :cols] = tall[f]
        rest = jnp.where(lane < HALO, turned(ahead, -HALO * f, 1), 0.0)
        rest = jnp.where(lane >= cols - HALO, turned(behind, cols - HALO - HALO * f, 1), rest)
        fields[f, :, cols:] = rest


def next_of(x, axis):
    return pltpu.roll(x, x.shape[axis] - 1, axis)


def previous_of(x, axis):
    return pltpu.roll(x, 1, axis)


def step_of(deepest):
    return COURANT * SPACING / jnp.sqrt(GRAVITY * jnp.maximum(deepest, DRY_FLOOR))


def fixed_parts(bed, opening):
    return tuple(
        (jnp.maximum(bed, next_of(bed, axis)), opening * next_of(opening, axis)) for axis in (0, 1)
    )


def face_flux(flow_old, surface, surf_high, bed_max, drag, opening, pull):
    flow_depth = jnp.maximum(surface, surf_high) - bed_max
    driving = jnp.maximum(flow_depth, 0.0)
    friction_depth = jnp.maximum(flow_depth, FLOW_FLOOR)
    driven = flow_old - (surf_high - surface) * pull * driving
    damping = 1.0 + drag * jnp.abs(flow_old) * jnp.exp(-7.0 / 3.0 * jnp.log(friction_depth))
    return opening * driven / damping


def advance(depth, flow_x, flow_y, bed, rough, faces, time_step):
    surface = depth + bed
    (bed_x, open_x), (bed_y, open_y) = faces
    drag = GRAVITY * time_step * rough
    pull = GRAVITY / SPACING * time_step
    rows_new = face_flux(flow_x, surface, next_of(surface, 0), bed_x, drag, open_x, pull)
    cols_new = face_flux(flow_y, surface, next_of(surface, 1), bed_y, drag, open_y, pull)
    change = previous_of(rows_new, 0) - rows_new + (previous_of(cols_new, 1) - cols_new)
    return jnp.maximum(depth + time_step / SPACING * change, 0.0), rows_new, cols_new


def lanes_of(shape):
    return lax.broadcasted_iota(jnp.int32, shape, len(shape) - 1)


def rows_of(shape):
    return lax.broadcasted_iota(jnp.int32, shape, len(shape) - 2)


def total(x, how):
    return how(how(x, axis=0, keepdims=True), axis=1, keepdims=True)


def merged(notes):
    if notes.shape[1] == BRIEF:
        return jnp.max(notes, axis=0, keepdims=True)
    head = notes[:, :128]
    lane = lanes_of(head.shape)
    out_lane = lanes_of((1, NOTE))
    place = rows_of((notes.shape[0], 1)).astype(jnp.float32)
    out = jnp.max(notes, axis=0, keepdims=True)
    for window in range(1, REACH + 1):
        keyed = jnp.max(jnp.where(lane == KEYS + window - 1, head, -1.0), axis=1, keepdims=True)
        best = keyed == jnp.max(keyed, axis=0, keepdims=True)
        first = jnp.min(jnp.where(best, place, 1e6), axis=0, keepdims=True)
        chosen = jnp.sum(jnp.where(place == first, notes, 0.0), axis=0, keepdims=True)
        for row in range(window + 1):
            tile, at = PLACES[window, row]
            start = 128 * tile + at
            here = (out_lane >= start) & (out_lane < start + FIELDS * (2 * window + 1))
            out = jnp.where(here, chosen, out)
    return out


def merge_kernel(notes, out):
    out[...] = jnp.broadcast_to(merged(notes[:, 0, :])[:, None, :], out.shape)


def turned(x, shift, axis):
    size = x.shape[axis]
    return pltpu.roll(x, shift % size, axis) if shift % size else x


def window_shape(window):
    return (8 if 2 * window < 8 else 16, 128)


def columns_of(shape, width):
    lane = lanes_of(shape)
    column = lane
    for f in range(1, FIELDS):
        column = jnp.where(lane >= width * f, lane - width * f, column)
    return column


def window_fields(note, window):
    width = 2 * window + 1
    shape = window_shape(window)
    row, lane = rows_of(shape), lanes_of(shape)
    column = columns_of(shape, width)
    folded = jnp.zeros(shape, jnp.float32)
    for i in range(window + 1):
        tile, at = PLACES[window, i]
        line = turned(note[:, 128 * tile : 128 * (tile + 1)], -at, 1)
        folded = jnp.where(row == i, jnp.broadcast_to(line, shape), folded)
    lower = turned(folded, window + 1, 0)
    lower = jnp.where(column <= window, turned(lower, -window, 1), turned(lower, window + 1, 1))
    packed = jnp.where(row <= window, folded, lower)
    inside = jnp.abs(column - window) + jnp.abs(row - window) <= window
    packed = jnp.where(inside, packed, 0.0)
    return [jnp.where(lane < width, turned(packed, -width * f, 1), 0.0) for f in range(FIELDS)]


def window_lines(saved, at_row, at_col, window):
    width = 2 * window + 1
    shape = window_shape(window)
    row, lane = rows_of(shape), lanes_of(shape)
    column = columns_of(shape, width)
    packed = jnp.zeros(shape, jnp.float32)
    top = at_row + 8 - window
    off = lax.rem(top, 8)
    height = shape[0] + 8
    for f in range(FIELDS):
        strip = saved[f, pl.ds(pl.multiple_of(top - off, 8), height), :]
        strip = pltpu.roll(strip, lax.rem(height - off, height), 0)[: shape[0]]
        shift = lax.rem(width * f + window - at_col + 2 * 256, 256)
        moved = pltpu.roll(strip, shift, 1)[:, :128]
        packed = jnp.where((lane >= width * f) & (lane < width * (f + 1)), moved, packed)
    lower = turned(packed, -(window + 1), 0)
    lower = jnp.where(column > window, turned(lower, window, 1), turned(lower, -(window + 1), 1))
    folded = jnp.where(jnp.abs(column - window) <= row, packed, lower)
    return [folded[i : i + 1] for i in range(window + 1)]


def run_kernel(tile, first, certain, reads, writes, *refs):
    if first:
        tall, after, before, fields, depth_out, flow_x_out, flow_y_out, note_out, guess_out, known_out = refs[:10]
        join(fields, tall, after, before)
    else:
        notes, guess_in, known_in, fields, depth_out, flow_x_out, flow_y_out, note_out, guess_out, known_out = refs[:10]
    state, faces, saved, times, depths, spots = refs[-6:]
    rows, cols = tile
    line_lane = lanes_of((1, 128))

    if first:
        known = jnp.int32(-1)
        guess_out[...] = jnp.full((1, 128), -1.0, jnp.float32)
    else:
        note = merged(notes[:, 0, :])
        true = note[:, :128]
        old = guess_in[...]
        wrong = jnp.where((true != old) & (line_lane < ITERS), line_lane.astype(jnp.float32), 1.0 * ITERS)
        miss = jnp.min(wrong).astype(jnp.int32)
        before = known_in[0]
        held = miss > before
        guess = true
        if reads:
            windows = {w: window_fields(note, w) for w in range(1, REACH + 1)}
            walls = {w: fixed_parts(parts[3], parts[5]) for w, parts in windows.items()}
            moving = {w: parts[:3] for w, parts in windows.items()}
            for stage in range(1, REACH + 1):
                level = jnp.max(jnp.where(line_lane == before + stage, guess, 0.0), axis=1, keepdims=True)
                time_step = step_of(level)
                for w in range(stage, REACH + 1):
                    moving[w] = advance(*moving[w], windows[w][3], windows[w][4], walls[w], time_step)
                shape = window_shape(stage)
                here = (rows_of(shape) == stage) & (lanes_of(shape) == stage)
                centre = total(jnp.where(here, moving[stage][0], 0.0), jnp.max)
                target = before + stage + 1
                use = held & (target > miss) & (line_lane == target) & (centre > 0.0)
                guess = jnp.where(use, centre, guess)
        known = miss
        if reads and not certain:
            known = jnp.where(held, jnp.maximum(before + REACH + 1, miss), miss)
        guess_out[...] = guess
        square = (16, 128)
        onto = rows_of(square) == lanes_of(square)
        spread = jnp.sum(jnp.where(onto, jnp.broadcast_to(guess, square), 0.0), axis=1, keepdims=True)
        times[...] = jnp.broadcast_to(step_of(spread), times.shape)
    known_out[0] = known if writes or first else jnp.int32(UNUSED)

    for f in range(3):
        state[f] = fields[f]
    bed, rough, opening = fields[3], fields[4], fields[5]
    for axis, (bed_max, both) in enumerate(fixed_parts(bed, opening)):
        faces[2 * axis] = bed_max
        faces[2 * axis + 1] = both
    last = fields.shape[1] - 8
    if writes:
        for f in range(3, FIELDS):
            saved[f, :8] = fields[f, last:]
            saved[f, 8:] = fields[f]
    depths[...] = jnp.full(depths.shape, -1.0, jnp.float32)

    def one_step(step, carry):
        depth, flow_x, flow_y = state[0], state[1], state[2]
        own = depth[:rows, :cols]
        deepest = total(own, jnp.max)
        depths[pl.ds(step, 1), :] = jnp.broadcast_to(deepest, (1, 128))

        @pl.when((step == known + 1) & writes)
        def _():
            for f in range(3):
                saved[f, :8] = state[f, last:]
                saved[f, 8:] = state[f]

        for j in range(REACH if writes else 0):

            @pl.when(step == known + 2 + j)
            def _():
                cell = (rows_of((rows, cols)) * cols + lanes_of((rows, cols))).astype(jnp.float32)
                spots[j] = jnp.min(jnp.where(own == deepest, cell, 1.0 * (rows * cols - 1))).astype(jnp.int32)

        time_step = step_of(deepest) if first else times[pl.ds(step, 1), :]
        new = advance(
            depth,
            flow_x,
            flow_y,
            fields[3],
            fields[4],
            ((faces[0], faces[1]), (faces[2], faces[3])),
            time_step,
        )
        for f in range(3):
            state[f] = new[f]
        return carry

    for j in range(REACH):
        spots[j] = 0
    lax.fori_loop(0, ITERS, one_step, 0)
    depth_out[...] = state[0, :rows, :cols]
    flow_x_out[...] = state[1, :rows, :cols]
    flow_y_out[...] = state[2, :rows, :cols]

    square = depths.shape
    onto = rows_of(square) == lanes_of(square)
    low = jnp.sum(jnp.where(onto, depths[...], 0.0), axis=0, keepdims=True)
    note = [low] + [jnp.zeros((1, 128), jnp.float32)] * (TILES - 1 if writes else 0)
    for j in range(REACH if writes else 0):
        window = j + 1
        key = jnp.max(jnp.where(line_lane == known + 1 + window, low, -1.0), axis=1, keepdims=True)
        note[0] = jnp.where(line_lane == KEYS + j, key, note[0])
        lines = window_lines(saved, spots[j] // cols, lax.rem(spots[j], cols), window)
        for i, line in enumerate(lines):
            tile, at = PLACES[window, i]
            here = (line_lane >= at) & (line_lane < at + FIELDS * (2 * window + 1))
            note[tile] = jnp.where(here, turned(line, at, 1), note[tile])
    note = jnp.concatenate(note, axis=1) if writes else low
    note_out[...] = jnp.broadcast_to(note[:, None, :], note_out.shape)


def per_device(depth, elevation, flow_x, flow_y, wet_mask, manning_class, manning_table):
    tile = depth.shape
    plane = ("core", "col")
    near_peers, far_peers = lax.axis_size("core") * lax.axis_size("col"), lax.axis_size("z")
    rows, cols = tile
    large = (rows + 2 * HALO, 2 * cols)
    vmem = pl.BlockSpec(memory_space=pltpu.VMEM)
    smem = pl.BlockSpec(memory_space=pltpu.SMEM)

    def f32(*shape):
        return jax.ShapeDtypeStruct(shape, jnp.float32)

    fields, first, last = pl.pallas_call(
        prepare_kernel,
        in_specs=[smem] + [pl.BlockSpec(memory_space=pl.ANY)] * 6,
        out_shape=(f32(FIELDS, *tile), f32(FIELDS, HALO, cols), f32(FIELDS, HALO, cols)),
        out_specs=(vmem,) * 3,
        scratch_shapes=[pltpu.VMEM((2, *tile), jnp.int32), pltpu.SemaphoreType.DMA((6,))],
        name="prepare",
    )(manning_table, depth, elevation, flow_x, flow_y, wet_mask, manning_class)
    up, down = neighbours(ROW)
    before, after = lax.ppermute(last, ROW, up), lax.ppermute(first, ROW, down)
    tall, first, last = pl.pallas_call(
        edge_kernel,
        in_specs=[vmem] * 3,
        out_shape=(f32(FIELDS, large[0], cols), f32(large[0], 128), f32(large[0], 128)),
        out_specs=(vmem,) * 3,
        name="edges",
    )(fields, after, before)
    up, down = neighbours("col")
    before, after = lax.ppermute(last, "col", up), lax.ppermute(first, "col", down)

    def everywhere(note):
        over_plane = lax.all_to_all(note, plane, 0, 0, tiled=True)
        merge = pl.pallas_call(merge_kernel, out_shape=f32(far_peers, 1, note.shape[2]), name="merge_notes")
        return lax.all_to_all(merge(over_plane), "z", 0, 0, tiled=True)

    def run(name, certain=False, reads=True, writes=True):
        first = name == "first_run"
        whole = (f32(FIELDS, *large),) if first else ()
        return pl.pallas_call(
            lambda *refs: run_kernel(tile, first, certain, reads, writes, *refs),
            in_specs=[vmem] * 3 if first else [vmem, vmem, smem, vmem],
            out_shape=(
                *whole,
                f32(*tile),
                f32(*tile),
                f32(*tile),
                f32(near_peers, 1, NOTE if writes else BRIEF),
                f32(1, 128),
                jax.ShapeDtypeStruct((1,), jnp.int32),
            ),
            out_specs=(vmem,) * (5 + len(whole)) + (smem,),
            scratch_shapes=[
                pltpu.VMEM((3, *large), jnp.float32),
                pltpu.VMEM((4, *large), jnp.float32),
                pltpu.VMEM((FIELDS, large[0] + 8, large[1]), jnp.float32),
                pltpu.VMEM((16, large[1]), jnp.float32),
                pltpu.VMEM((16, 128), jnp.float32),
                pltpu.SMEM((REACH,), jnp.int32),
            ],
            name=name,
        )

    def settled(notes, guess):
        true = jnp.max(notes[:, 0, :ITERS], axis=0)
        return jnp.all(true == guess[0, :ITERS])

    fields, *result, note, guess, known = run("first_run", reads=False, writes=False)(tall, after, before)
    later = run("later_run")
    for again in (
        run("second_run", certain=True, reads=False),
        run("third_run", certain=True),
        later,
        run("check_run", writes=False),
    ):
        *result, note, guess, known = again(everywhere(note), guess, known, fields)
    notes = everywhere(note)
    done = settled(notes, guess)
    notes = jnp.pad(notes, ((0, 0), (0, 0), (0, NOTE - BRIEF)))

    def unsettled(carry):
        return jnp.logical_not(carry[1]) & (carry[0] <= ITERS)

    def one_round(carry):
        count, _, notes, guess, known, _ = carry
        *result, note, guess, known = later(notes, guess, known, fields)
        notes = everywhere(note)
        return count + 1, settled(notes, guess), notes, guess, known, tuple(result)

    carry = (jnp.int32(0), done, notes, guess, known, tuple(result))
    return lax.while_loop(unsettled, one_round, carry)[-1]


def solution(mesh):
    rows, cols = mesh.devices.shape
    split = jax.sharding.Mesh(mesh.devices.reshape(rows // 2, 2, cols), (*ROW, "col"))
    block = P(ROW, "col")
    return jax.shard_map(
        per_device,
        mesh=split,
        in_specs=(block, block, block, block, block, block, P()),
        out_specs=(block, block, block),
        check_vma=False,
    )
```
